32 devices in a mesh: row: 4 (over z), col: 8 (over y, x, core).
Axes of the slice: x: 2, y: 2, z: 4, core: 2. Of those that a mesh axis runs over, the one named last changes fastest.
Arguments:
- rhs_panels: float32 [3, 4, 8, 64, 256], P(None, 'row', 'col'), may hold values from -6 to 6
- inverse_diag: bfloat16 [3, 4, 8, 256, 256], P(None, 'row', 'col'), may hold values from -0.375 to 0.375
- factor_blocks: bfloat16 [3, 4, 80, 256, 256], P(None, 'row', 'col'), may hold values from -0.078125 to 0.078125
- block_target: int32 [3, 4, 80], P(None, 'row', 'col'), may hold values from 0 to 3, as said below
- block_source: int32 [3, 4, 80], P(None, 'row', 'col'), may hold values from 0 to 7, as said below
Outputs:
- solution: float32 [3, 4, 8, 64, 256], P(None, 'row', 'col')
The draws below stay inside these ranges and needn't reach their ends.
Inputs may be any that keep to these rules, and one draw needn't show every extreme that they name: (block_target[p, r, q] - r) modulo 4 is below 2, or equals 2, or equals 3; each of 1, 2 and 3 occurs. (block_source[p, r, q] - q // 10) modulo 8 is below 2, or equals 4, or equals 7; each of 1, 4 and 7 occurs.
All inputs are finite; a program needn't handle non-finite values.
Results may differ from the reference program's by a relative error of at most 0.014.
Values may be sent and summed in bfloat16 or wider, within the bound.
A program may use at most 64 MiB of HBM per device.

```python
import jax
import jax.numpy as jnp
from jax import lax

BS = 256
NRHS = 64
LEVELS = 3
WINDOW = 2
SLOTS = 10
PAIRS = 3
N_ROW = 4
N_COL = 8


def offset_choices(window, count):
    values = sorted(set(list(range(window)) + [count // 2, count - 1]))
    return values


def draw_offsets(key, count):
    values = offset_choices(WINDOW, count)
    table = jnp.array(values, dtype=jnp.int32)
    picks = jax.random.randint(key, (PAIRS, N_ROW, N_COL * SLOTS), 0, len(values)).astype(jnp.int32)
    offsets = table[picks]
    offsets = offsets.at[0, 0, 0].set(count // 2)
    offsets = offsets.at[0, 1, 0].set(count - 1)
    offsets = offsets.at[0, 2, 0].set(WINDOW - 1)
    return offsets.astype(jnp.int32)


def draw_block_target(key, part):
    offsets = draw_offsets(jax.random.fold_in(key, 11), N_ROW)
    rows_here = jnp.arange(N_ROW, dtype=jnp.int32)[None, :, None]
    return ((rows_here + offsets) % N_ROW).astype(jnp.int32)


def draw_block_source(key, part):
    offsets = draw_offsets(jax.random.fold_in(key, 23), N_COL)
    cols_here = (jnp.arange(N_COL * SLOTS, dtype=jnp.int32) // SLOTS)[None, None, :]
    return ((cols_here + offsets) % N_COL).astype(jnp.int32)


def level_of(key, dims, cuts, low, largest):
    loudness = 1.0
    for dim, parts in cuts:
        draws = jax.random.uniform(jax.random.fold_in(jax.random.fold_in(key, 6), dim), (parts,), jnp.float32, low / len(cuts), largest / len(cuts))
        loudness = loudness * jnp.repeat(jnp.exp(draws), dims[dim] // parts).reshape((-1,) + (1,) * (len(dims) - 1 - dim))
    return loudness


def centred(stream_key, shape, width, limit, cuts=(), held_as=jnp.bfloat16):
    values = jax.random.normal(stream_key, shape, jnp.float32) * width
    if len(cuts) > 0:
        values = level_of(stream_key, shape, cuts, -0.22, 0.18) * values
    return jnp.clip(values, min=-limit, max=limit).astype(held_as)


def setup_inputs(seed: int = 0) -> dict:
    key_list = jax.random.split(jax.random.key(seed), 6)
    rhs_panels = centred(key_list[0], (LEVELS, N_ROW, N_COL, NRHS, BS), 1.0, 6.0, ((1, 4), (2, 8)), jnp.float32)
    inverse_diag = centred(key_list[1], (LEVELS, N_ROW, N_COL, BS, BS), BS ** -0.5, 0.375, ((1, 4), (2, 8)))
    factor_blocks = centred(key_list[2], (PAIRS, N_ROW, N_COL * SLOTS, BS, BS), (2 * BS * SLOTS) ** -0.5, 0.078125, ((1, 4), (2, 8)))
    block_target = draw_block_target(jax.random.fold_in(key_list[5], 71), 0)
    block_source = draw_block_source(jax.random.fold_in(key_list[5], 71), 0)
    return {"rhs_panels": rhs_panels, "inverse_diag": inverse_diag, "factor_blocks": factor_blocks, "block_target": block_target, "block_source": block_source}


def pair_table(levels):
    return [(target_lvl, source_lvl) for target_lvl in range(1, levels) for source_lvl in range(target_lvl)]


def reference(rhs_panels, inverse_diag, factor_blocks, block_target, block_source):
    pair_list = pair_table(LEVELS)
    blocks = factor_blocks.reshape(PAIRS, N_ROW, N_COL, SLOTS, BS, BS)
    targets = block_target.reshape(PAIRS, N_ROW, N_COL, SLOTS).astype(jnp.int32)
    sources = block_source.reshape(PAIRS, N_ROW, N_COL, SLOTS).astype(jnp.int32)
    row_iota = jnp.arange(N_ROW, dtype=jnp.int32)
    col_iota = jnp.arange(N_COL, dtype=jnp.int32)
    forward = []
    forward_bf = []
    for current in range(LEVELS):
        residual = rhs_panels[current]
        if current > 0:
            chosen = [pair_idx for pair_idx, pair_info in enumerate(pair_list) if pair_info[0] == current]
            scanned_in = tuple((blocks[pair_idx], targets[pair_idx], sources[pair_idx], forward_bf[pair_list[pair_idx][1]]) for pair_idx in chosen)

            def step_row(running, scanned):
                term_sum = jnp.zeros((N_COL, N_ROW, NRHS, BS), jnp.float32)
                for row_blocks, row_targets, row_sources, row_panels in scanned:
                    picked = row_panels[row_sources]
                    products = jnp.einsum("csnb,csab->csna", picked.astype(jnp.float32), row_blocks.astype(jnp.float32), precision=lax.Precision.HIGHEST)
                    onehot = (row_targets[:, :, None] == row_iota[None, None, :]).astype(jnp.float32)
                    term_sum = term_sum + jnp.einsum("cst,csna->ctna", onehot, products, precision=lax.Precision.HIGHEST)
                rounded = lax.optimization_barrier(term_sum.astype(jnp.bfloat16)).astype(jnp.float32)
                return running + rounded, None

            total_init = jnp.zeros((N_COL, N_ROW, NRHS, BS), jnp.float32)
            summed, unused = lax.scan(step_row, total_init, scanned_in)
            residual = residual - jnp.transpose(summed, (1, 0, 2, 3))
        reduced = residual.astype(jnp.bfloat16)
        panel_now = jnp.einsum("rcnb,rcab->rcna", reduced.astype(jnp.float32), inverse_diag[current].astype(jnp.float32), precision=lax.Precision.HIGHEST)
        forward.append(panel_now)
        forward_bf.append(panel_now.astype(jnp.bfloat16))
    solutions = [None] * LEVELS
    backward_bf = [None] * LEVELS
    for current in reversed(range(LEVELS)):
        residual = forward[current]
        if current < LEVELS - 1:
            chosen = [pair_idx for pair_idx, pair_info in enumerate(pair_list) if pair_info[1] == current]
            dst_levels = [pair_list[pair_idx][0] for pair_idx in chosen]
            scanned_in = tuple((blocks[pair_idx], targets[pair_idx], sources[pair_idx]) for pair_idx in chosen)

            def back_row(scanned):
                term_sum = jnp.zeros((N_COL, N_COL, NRHS, BS), jnp.float32)
                for member, dst_level in zip(scanned, dst_levels):
                    row_blocks, row_targets, row_sources = member
                    picked = backward_bf[dst_level][row_targets, col_iota[:, None]]
                    products = jnp.einsum("csnb,csba->csna", picked.astype(jnp.float32), row_blocks.astype(jnp.float32), precision=lax.Precision.HIGHEST)
                    onehot = (row_sources[:, :, None] == col_iota[None, None, :]).astype(jnp.float32)
                    term_sum = term_sum + jnp.einsum("cse,csna->cena", onehot, products, precision=lax.Precision.HIGHEST)
                rounded = lax.optimization_barrier(term_sum.astype(jnp.bfloat16)).astype(jnp.float32)
                return jnp.sum(rounded, axis=0)

            summed = lax.map(back_row, scanned_in)
            residual = residual - summed
        reduced = residual.astype(jnp.bfloat16)
        answer = jnp.einsum("rcnb,rcba->rcna", reduced.astype(jnp.float32), inverse_diag[current].astype(jnp.float32), precision=lax.Precision.HIGHEST)
        solutions[current] = answer
        backward_bf[current] = answer.astype(jnp.bfloat16)
    return jnp.stack(solutions)
```

```python
import functools

import jax
import jax.numpy as jnp
from jax import lax
from jax.experimental import pallas as pl
from jax.experimental.pallas import tpu as pltpu
from jax.sharding import PartitionSpec as P

WINDOW = 2
MESH = pl.DeviceIdType.MESH


def pair_table(levels):
    return [(d, s) for d in range(1, levels) for s in range(d)]


def offset_choices(window, count):
    return sorted(set(list(range(window)) + [count // 2, count - 1]))


def kernel(
    n_row,
    n_col,
    rhs_hbm,
    inv_hbm,
    fac_hbm,
    tgt_ref,
    src_ref,
    out_ref,
    rhs,
    inv,
    fac,
    ycol,
    brow,
    fpart,
    frecv,
    bpart,
    brecv,
    yfull,
    facc,
    bacc,
    ftab,
    btab,
    rhs_sem,
    inv_sem,
    fac_sem,
    send_sem,
    recv_sem,
):
    levels = rhs.shape[0]
    slots = fac.shape[1]
    nrhs = rhs.shape[1]
    pairs = pair_table(levels)
    row_vals = offset_choices(WINDOW, n_row)
    col_vals = offset_choices(WINDOW, n_col)
    row_w, col_w = len(row_vals), len(col_vals)
    me_r, me_c = lax.axis_index("row"), lax.axis_index("col")

    def row_dev(steps):
        return {"row": lax.rem(me_r + (steps + n_row), n_row)}

    def col_dev(steps):
        return {"col": lax.rem(me_c + (steps + n_col), n_col)}

    loads = {}
    for k in range(levels):
        loads["rhs", k] = pltpu.make_async_copy(rhs_hbm.at[k, 0, 0], rhs.at[k], rhs_sem.at[k])
        loads["inv", k] = pltpu.make_async_copy(inv_hbm.at[k, 0, 0], inv.at[k], inv_sem.at[k])
    for p in range(len(pairs)):
        loads["fac", p] = pltpu.make_async_copy(fac_hbm.at[p, 0], fac.at[p], fac_sem.at[p])
    loads["rhs", 0].start()
    loads["inv", 0].start()
    loads["fac", 0].start()
    for k in range(1, levels):
        loads["rhs", k].start()
        loads["inv", k].start()
    for p in range(1, len(pairs)):
        loads["fac", p].start()
    loaded = set()

    def need(*key):
        if key not in loaded:
            loads[key].wait()
            loaded.add(key)

    barrier = pltpu.get_barrier_semaphore()
    for v in row_vals[1:]:
        pl.semaphore_signal(barrier, inc=1, device_id=row_dev(v), device_id_type=MESH)
    for v in col_vals[1:]:
        pl.semaphore_signal(barrier, inc=1, device_id=col_dev(v), device_id_type=MESH)

    sends = []

    def send(phase, slot, src, dst, device):
        copy = pltpu.make_async_remote_copy(
            src_ref=src,
            dst_ref=dst,
            send_sem=send_sem.at[phase, slot],
            recv_sem=recv_sem.at[phase, slot],
            device_id=device,
            device_id_type=MESH,
        )
        copy.start()
        sends.append(copy)
        return copy

    def dot_t(a, b):
        return lax.dot_general(a, b, (((1,), (1,)), ((), ())), preferred_element_type=jnp.float32)

    def dot_n(a, b):
        return jnp.dot(a, b, preferred_element_type=jnp.float32)

    def order(vals):
        return [k for k in (2, 3, 1) if k < len(vals)] + list(range(4, len(vals)))

    def product(p, panels, table, width, dot):
        need("fac", p)
        total = None
        for q in range(slots):
            stacked = jnp.concatenate([panels[table[p, q, j]] for j in range(width)], axis=0)
            term = dot(stacked, fac[p, q])
            total = term if total is None else total + term
        return total

    def spread(phase, vals, device, total, part, recv):
        copies = []
        for k in order(vals):
            part[k] = total[k * nrhs : (k + 1) * nrhs].astype(jnp.bfloat16)
            copies.append(send(phase, k, part.at[k], recv.at[k], device(vals[k])))
        return copies, total[:nrhs].astype(jnp.bfloat16).astype(jnp.float32)

    def collect(copies, recv, own, width):
        for copy in copies:
            copy.wait_recv()
        for k in range(1, width):
            own = own + recv[k].astype(jnp.float32)
        return own

    def share(phase, vals, device, panels):
        return [
            send(phase, k, panels.at[0], panels.at[k], device(-vals[k])) for k in order(vals)
        ]

    need("rhs", 0)
    need("inv", 0)
    y = dot_t(rhs[0].astype(jnp.bfloat16), inv[0])
    yfull[0] = y
    ycol[0][0] = y.astype(jnp.bfloat16)
    pl.semaphore_wait(barrier, row_w + col_w - 2)
    phase = 0
    copies = share(phase, col_vals, col_dev, ycol[0])

    for lvl in range(levels - 1):
        ycol[lvl][col_w] = jnp.zeros((nrhs, rhs.shape[2]), jnp.bfloat16)
        brow[lvl + 1][row_w] = jnp.zeros((nrhs, rhs.shape[2]), jnp.bfloat16)
    for p in range(len(pairs)):
        for q in range(slots):
            off_r = tgt_ref[p, 0, q] - me_r
            off_c = src_ref[p, 0, q] - me_c
            off_r = jnp.where(off_r < 0, off_r + n_row, off_r)
            off_c = jnp.where(off_c < 0, off_c + n_col, off_c)
            pos_r = jnp.int32(0)
            for k in range(1, row_w):
                pos_r = jnp.where(off_r == row_vals[k], k, pos_r)
            pos_c = jnp.int32(0)
            for k in range(1, col_w):
                pos_c = jnp.where(off_c == col_vals[k], k, pos_c)
            for k in range(row_w):
                ftab[p, q, k] = jnp.where(pos_r == k, pos_c, col_w)
            for k in range(col_w):
                btab[p, q, k] = jnp.where(pos_c == k, pos_r, row_w)

    for k in range(1, levels):
        total = None
        for p, (d, s) in enumerate(pairs):
            if d == k and s == k - 1:
                for copy in copies:
                    copy.wait_recv()
                total = product(p, ycol[s], ftab, row_w, dot_t)
        if k > 1:
            total = total + facc[k]
        phase += 1
        copies, own = spread(phase, row_vals, row_dev, total, fpart.at[k], frecv.at[k])
        for p, (d, s) in enumerate(pairs):
            if s == k - 1 and d > k:
                later = product(p, ycol[s], ftab, row_w, dot_t)
                facc[d] = later if s == 0 else facc[d] + later
        need("rhs", k)
        need("inv", k)
        fsum = collect(copies, frecv.at[k], own, row_w)
        y = dot_t((rhs[k] - fsum).astype(jnp.bfloat16), inv[k])
        if k < levels - 1:
            yfull[k] = y
            ycol[k][0] = y.astype(jnp.bfloat16)
            phase += 1
            copies = share(phase, col_vals, col_dev, ycol[k])

    top = levels - 1
    answer = dot_n(y.astype(jnp.bfloat16), inv[top])
    brow[top][0] = answer.astype(jnp.bfloat16)
    phase += 1
    copies = share(phase, row_vals, row_dev, brow[top])
    out_ref[top, 0, 0] = answer
    for k in reversed(range(top)):
        total = None
        for p, (d, s) in enumerate(pairs):
            if s == k and d == k + 1:
                for copy in copies:
                    copy.wait_recv()
                total = product(p, brow[d], btab, col_w, dot_n)
        if k + 1 < top:
            total = total + bacc[k]
        phase += 1
        copies, own = spread(phase, col_vals, col_dev, total, bpart.at[k], brecv.at[k])
        for p, (d, s) in enumerate(pairs):
            if d == k + 1 and s < k:
                later = product(p, brow[d], btab, col_w, dot_n)
                bacc[s] = later if d == top else bacc[s] + later
        bsum = collect(copies, brecv.at[k], own, col_w)
        answer = dot_n((yfull[k] - bsum).astype(jnp.bfloat16), inv[k])
        if k > 0:
            brow[k][0] = answer.astype(jnp.bfloat16)
            phase += 1
            copies = share(phase, row_vals, row_dev, brow[k])
        out_ref[k, 0, 0] = answer
    for copy in sends:
        copy.wait_send()


def shards(n_row, n_col, rhs, inv, fac, tgt, src):
    levels, nrhs, size = rhs.shape[0], rhs.shape[3], rhs.shape[4]
    pairs, slots = fac.shape[0], fac.shape[2]
    row_w = len(offset_choices(WINDOW, n_row))
    col_w = len(offset_choices(WINDOW, n_col))
    width = max(row_w, col_w)
    phases = 4 * (levels - 1)
    bf, f32 = jnp.bfloat16, jnp.float32
    return pl.pallas_call(
        functools.partial(kernel, n_row, n_col),
        out_shape=jax.ShapeDtypeStruct(rhs.shape, f32),
        in_specs=[pl.BlockSpec(memory_space=pl.ANY)] * 3
        + [pl.BlockSpec(memory_space=pltpu.SMEM)] * 2,
        out_specs=pl.BlockSpec(memory_space=pltpu.VMEM),
        scratch_shapes=[
            pltpu.VMEM((levels, nrhs, size), f32),
            pltpu.VMEM((levels, size, size), bf),
            pltpu.VMEM((pairs, slots, size, size), bf),
            [pltpu.VMEM((col_w + 1, nrhs, size), bf)] * (levels - 1),
            [pltpu.VMEM((row_w + 1, nrhs, size), bf)] * levels,
            pltpu.VMEM((levels, row_w, nrhs, size), bf),
            pltpu.VMEM((levels, row_w, nrhs, size), bf),
            pltpu.VMEM((levels - 1, col_w, nrhs, size), bf),
            pltpu.VMEM((levels - 1, col_w, nrhs, size), bf),
            pltpu.VMEM((levels - 1, nrhs, size), f32),
            pltpu.VMEM((levels, row_w * nrhs, size), f32),
            pltpu.VMEM((levels - 1, col_w * nrhs, size), f32),
            pltpu.SMEM((pairs, slots, row_w), jnp.int32),
            pltpu.SMEM((pairs, slots, col_w), jnp.int32),
            pltpu.SemaphoreType.DMA((levels,)),
            pltpu.SemaphoreType.DMA((levels,)),
            pltpu.SemaphoreType.DMA((pairs,)),
            pltpu.SemaphoreType.DMA((phases, width)),
            pltpu.SemaphoreType.DMA((phases, width)),
        ],
        compiler_params=pltpu.CompilerParams(collective_id=0, has_side_effects=True),
    )(rhs, inv, fac, tgt, src)


def solution(mesh):
    placed = (
        P(None, "row", "col", None, None),
        P(None, "row", "col", None, None),
        P(None, "row", "col", None, None),
        P(None, "row", "col"),
        P(None, "row", "col"),
    )
    return jax.shard_map(
        functools.partial(shards, mesh.shape["row"], mesh.shape["col"]),
        mesh=mesh,
        in_specs=placed,
        out_specs=P(None, "row", "col", None, None),
        check_vma=False,
    )
```

```python
import functools

import jax
import jax.numpy as jnp
from jax import lax
from jax.experimental import pallas as pl
from jax.experimental.pallas import tpu as pltpu
from jax.sharding import PartitionSpec as P

WINDOW = 2
MESH = pl.DeviceIdType.MESH


def pair_table(levels):
    return [(d, s) for d in range(1, levels) for s in range(d)]


def offset_choices(window, count):
    return sorted(set(list(range(window)) + [count // 2, count - 1]))


def kernel(
    n_row,
    n_col,
    rhs_hbm,
    inv_hbm,
    fac_hbm,
    tgt_hbm,
    src_hbm,
    out_ref,
    rhs,
    inv,
    fac,
    ycol,
    brow,
    fpart,
    frecv,
    bpart,
    brecv,
    yfull,
    facc,
    bacc,
    tgt_ref,
    src_ref,
    ftab,
    btab,
    idx_sem,
    rhs_sem,
    inv_sem,
    fac_sem,
    send_sem,
    recv_sem,
):
    levels = rhs.shape[0]
    slots = fac.shape[1]
    nrhs = rhs.shape[1]
    pairs = pair_table(levels)
    row_vals = offset_choices(WINDOW, n_row)
    col_vals = offset_choices(WINDOW, n_col)
    row_w, col_w = len(row_vals), len(col_vals)
    me_r, me_c = lax.axis_index("row"), lax.axis_index("col")

    def row_dev(steps):
        return {"row": lax.rem(me_r + (steps + n_row), n_row)}

    def col_dev(steps):
        return {"col": lax.rem(me_c + (steps + n_col), n_col)}

    barrier = pltpu.get_barrier_semaphore()
    for v in row_vals[1:]:
        pl.semaphore_signal(barrier, inc=1, device_id=row_dev(v), device_id_type=MESH)
    for v in col_vals[1:]:
        pl.semaphore_signal(barrier, inc=1, device_id=col_dev(v), device_id_type=MESH)

    loads = {}
    for k in range(levels):
        loads["rhs", k] = pltpu.make_async_copy(rhs_hbm.at[k, 0, 0], rhs.at[k], rhs_sem.at[k])
        loads["inv", k] = pltpu.make_async_copy(inv_hbm.at[k, 0, 0], inv.at[k], inv_sem.at[k])
    for p in range(len(pairs)):
        loads["fac", p] = pltpu.make_async_copy(fac_hbm.at[p, 0], fac.at[p], fac_sem.at[p])
    loads["rhs", 0].start()
    loads["inv", 0].start()
    loads["tgt", 0] = pltpu.make_async_copy(tgt_hbm, tgt_ref, idx_sem.at[0])
    loads["src", 0] = pltpu.make_async_copy(src_hbm, src_ref, idx_sem.at[1])
    loads["tgt", 0].start()
    loads["src", 0].start()
    loads["fac", 0].start()
    for k in range(1, levels):
        loads["rhs", k].start()
        loads["inv", k].start()
    for p in range(1, len(pairs)):
        loads["fac", p].start()
    loaded = set()

    def need(*key):
        if key not in loaded:
            loads[key].wait()
            loaded.add(key)

    sends = []

    def send(phase, slot, src, dst, device):
        copy = pltpu.make_async_remote_copy(
            src_ref=src,
            dst_ref=dst,
            send_sem=send_sem.at[phase, slot],
            recv_sem=recv_sem.at[phase, slot],
            device_id=device,
            device_id_type=MESH,
        )
        copy.start()
        sends.append(copy)
        return copy

    def dot_t(a, b):
        return lax.dot_general(a, b, (((1,), (1,)), ((), ())), preferred_element_type=jnp.float32)

    def dot_n(a, b):
        return jnp.dot(a, b, preferred_element_type=jnp.float32)

    def order(vals):
        return [k for k in (2, 3, 1) if k < len(vals)] + list(range(4, len(vals)))

    def product(p, panels, table, width, dot):
        need("fac", p)
        total = None
        for q in range(slots):
            stacked = jnp.concatenate([panels[table[p, q, j]] for j in range(width)], axis=0)
            term = dot(stacked, fac[p, q])
            total = term if total is None else total + term
        return total

    def spread(phase, vals, device, total, part, recv):
        copies = []
        for k in order(vals):
            part[k] = total[k * nrhs : (k + 1) * nrhs].astype(jnp.bfloat16)
            copies.append(send(phase, k, part.at[k], recv.at[k], device(vals[k])))
        return copies, total[:nrhs].astype(jnp.bfloat16).astype(jnp.float32)

    def collect(copies, recv, own, width):
        for copy in copies:
            copy.wait_recv()
        for k in range(1, width):
            own = own + recv[k].astype(jnp.float32)
        return own

    def share(phase, vals, device, panels):
        return [
            send(phase, k, panels.at[0], panels.at[k], device(-vals[k])) for k in order(vals)
        ]

    need("rhs", 0)
    need("inv", 0)
    y = dot_t(rhs[0].astype(jnp.bfloat16), inv[0])
    yfull[0] = y
    ycol[0][0] = y.astype(jnp.bfloat16)
    pl.semaphore_wait(barrier, row_w + col_w - 2)
    phase = 0
    copies = share(phase, col_vals, col_dev, ycol[0])

    for lvl in range(levels - 1):
        ycol[lvl][col_w] = jnp.zeros((nrhs, rhs.shape[2]), jnp.bfloat16)
        brow[lvl + 1][row_w] = jnp.zeros((nrhs, rhs.shape[2]), jnp.bfloat16)
    need("tgt", 0)
    need("src", 0)
    for p in range(len(pairs)):
        for q in range(slots):
            off_r = tgt_ref[p, 0, q] - me_r
            off_c = src_ref[p, 0, q] - me_c
            off_r = jnp.where(off_r < 0, off_r + n_row, off_r)
            off_c = jnp.where(off_c < 0, off_c + n_col, off_c)
            pos_r = jnp.int32(0)
            for k in range(1, row_w):
                pos_r = jnp.where(off_r == row_vals[k], k, pos_r)
            pos_c = jnp.int32(0)
            for k in range(1, col_w):
                pos_c = jnp.where(off_c == col_vals[k], k, pos_c)
            for k in range(row_w):
                ftab[p, q, k] = jnp.where(pos_r == k, pos_c, col_w)
            for k in range(col_w):
                btab[p, q, k] = jnp.where(pos_c == k, pos_r, row_w)

    for k in range(1, levels):
        total = None
        for p, (d, s) in enumerate(pairs):
            if d == k and s == k - 1:
                for copy in copies:
                    copy.wait_recv()
                total = product(p, ycol[s], ftab, row_w, dot_t)
        if k > 1:
            total = total + facc[k]
        phase += 1
        copies, own = spread(phase, row_vals, row_dev, total, fpart.at[k], frecv.at[k])
        for p, (d, s) in enumerate(pairs):
            if s == k - 1 and d > k:
                later = product(p, ycol[s], ftab, row_w, dot_t)
                facc[d] = later if s == 0 else facc[d] + later
        need("rhs", k)
        need("inv", k)
        fsum = collect(copies, frecv.at[k], own, row_w)
        y = dot_t((rhs[k] - fsum).astype(jnp.bfloat16), inv[k])
        if k < levels - 1:
            yfull[k] = y
            ycol[k][0] = y.astype(jnp.bfloat16)
            phase += 1
            copies = share(phase, col_vals, col_dev, ycol[k])

    top = levels - 1
    answer = dot_n(y.astype(jnp.bfloat16), inv[top])
    brow[top][0] = answer.astype(jnp.bfloat16)
    phase += 1
    copies = share(phase, row_vals, row_dev, brow[top])
    out_ref[top, 0, 0] = answer
    for k in reversed(range(top)):
        total = None
        for p, (d, s) in enumerate(pairs):
            if s == k and d == k + 1:
                for copy in copies:
                    copy.wait_recv()
                total = product(p, brow[d], btab, col_w, dot_n)
        if k + 1 < top:
            total = total + bacc[k]
        phase += 1
        copies, own = spread(phase, col_vals, col_dev, total, bpart.at[k], brecv.at[k])
        for p, (d, s) in enumerate(pairs):
            if d == k + 1 and s < k:
                later = product(p, brow[d], btab, col_w, dot_n)
                bacc[s] = later if d == top else bacc[s] + later
        bsum = collect(copies, brecv.at[k], own, col_w)
        answer = dot_n((yfull[k] - bsum).astype(jnp.bfloat16), inv[k])
        if k > 0:
            brow[k][0] = answer.astype(jnp.bfloat16)
            phase += 1
            copies = share(phase, row_vals, row_dev, brow[k])
        out_ref[k, 0, 0] = answer
    for copy in sends:
        copy.wait_send()


def shards(n_row, n_col, rhs, inv, fac, tgt, src):
    levels, nrhs, size = rhs.shape[0], rhs.shape[3], rhs.shape[4]
    pairs, slots = fac.shape[0], fac.shape[2]
    row_w = len(offset_choices(WINDOW, n_row))
    col_w = len(offset_choices(WINDOW, n_col))
    width = max(row_w, col_w)
    phases = 4 * (levels - 1)
    bf, f32 = jnp.bfloat16, jnp.float32
    return pl.pallas_call(
        functools.partial(kernel, n_row, n_col),
        out_shape=pltpu.VMEM(rhs.shape, f32),
        in_specs=[pl.BlockSpec(memory_space=pl.ANY)] * 5,
        out_specs=pl.BlockSpec(memory_space=pltpu.VMEM),
        scratch_shapes=[
            pltpu.VMEM((levels, nrhs, size), f32),
            pltpu.VMEM((levels, size, size), bf),
            pltpu.VMEM((pairs, slots, size, size), bf),
            [pltpu.VMEM((col_w + 1, nrhs, size), bf)] * (levels - 1),
            [pltpu.VMEM((row_w + 1, nrhs, size), bf)] * levels,
            pltpu.VMEM((levels, row_w, nrhs, size), bf),
            pltpu.VMEM((levels, row_w, nrhs, size), bf),
            pltpu.VMEM((levels - 1, col_w, nrhs, size), bf),
            pltpu.VMEM((levels - 1, col_w, nrhs, size), bf),
            pltpu.VMEM((levels - 1, nrhs, size), f32),
            pltpu.VMEM((levels, row_w * nrhs, size), f32),
            pltpu.VMEM((levels - 1, col_w * nrhs, size), f32),
            pltpu.SMEM(tgt.shape, jnp.int32),
            pltpu.SMEM(src.shape, jnp.int32),
            pltpu.SMEM((pairs, slots, row_w), jnp.int32),
            pltpu.SMEM((pairs, slots, col_w), jnp.int32),
            pltpu.SemaphoreType.DMA((2,)),
            pltpu.SemaphoreType.DMA((levels,)),
            pltpu.SemaphoreType.DMA((levels,)),
            pltpu.SemaphoreType.DMA((pairs,)),
            pltpu.SemaphoreType.DMA((phases, width)),
            pltpu.SemaphoreType.DMA((phases, width)),
        ],
        compiler_params=pltpu.CompilerParams(collective_id=0, has_side_effects=True),
    )(rhs, inv, fac, tgt, src)


def solution(mesh):
    placed = (
        P(None, "row", "col", None, None),
        P(None, "row", "col", None, None),
        P(None, "row", "col", None, None),
        P(None, "row", "col"),
        P(None, "row", "col"),
    )
    return jax.shard_map(
        functools.partial(shards, mesh.shape["row"], mesh.shape["col"]),
        mesh=mesh,
        in_specs=placed,
        out_specs=P(None, "row", "col", None, None),
        check_vma=False,
    )
```

```python
import functools

import jax
import jax.numpy as jnp
from jax import lax
from jax.experimental import pallas as pl
from jax.experimental.pallas import tpu as pltpu
from jax.sharding import PartitionSpec as P

WINDOW = 2
STREAMS = 2
MESH = pl.DeviceIdType.MESH


def pair_table(levels):
    return [(d, s) for d in range(1, levels) for s in range(d)]


def offset_choices(window, count):
    return sorted(set(list(range(window)) + [count // 2, count - 1]))


def kernel(
    n_row,
    n_col,
    rhs_hbm,
    inv_hbm,
    fac_hbm,
    tgt_hbm,
    src_hbm,
    out_ref,
    rhs,
    inv,
    fac,
    ycol,
    brow,
    fpart,
    frecv,
    bpart,
    brecv,
    yfull,
    facc,
    bacc,
    tgt_ref,
    src_ref,
    ftab,
    btab,
    idx_sem,
    rhs_sem,
    inv_sem,
    fac_sem,
    send_sem,
    recv_sem,
):
    levels = rhs.shape[0]
    slots = fac.shape[1]
    streams = len(ycol)
    rows = rhs.shape[1] // streams
    pairs = pair_table(levels)
    row_vals = offset_choices(WINDOW, n_row)
    col_vals = offset_choices(WINDOW, n_col)
    row_w, col_w = len(row_vals), len(col_vals)
    me_r, me_c = lax.axis_index("row"), lax.axis_index("col")

    def row_dev(steps):
        return {"row": lax.rem(me_r + (steps + n_row), n_row)}

    def col_dev(steps):
        return {"col": lax.rem(me_c + (steps + n_col), n_col)}

    barrier = pltpu.get_barrier_semaphore()
    for v in row_vals[1:]:
        pl.semaphore_signal(barrier, inc=1, device_id=row_dev(v), device_id_type=MESH)
    for v in col_vals[1:]:
        pl.semaphore_signal(barrier, inc=1, device_id=col_dev(v), device_id_type=MESH)

    loads = {}
    for k in range(levels):
        loads["rhs", k] = pltpu.make_async_copy(rhs_hbm.at[k, 0, 0], rhs.at[k], rhs_sem.at[k])
        loads["inv", k] = pltpu.make_async_copy(inv_hbm.at[k, 0, 0], inv.at[k], inv_sem.at[k])
    for p in range(len(pairs)):
        loads["fac", p] = pltpu.make_async_copy(fac_hbm.at[p, 0], fac.at[p], fac_sem.at[p])
    loads["rhs", 0].start()
    loads["inv", 0].start()
    loads["tgt", 0] = pltpu.make_async_copy(tgt_hbm, tgt_ref, idx_sem.at[0])
    loads["src", 0] = pltpu.make_async_copy(src_hbm, src_ref, idx_sem.at[1])
    loads["tgt", 0].start()
    loads["src", 0].start()
    loads["fac", 0].start()
    for k in range(1, levels):
        loads["rhs", k].start()
        loads["inv", k].start()
    for p in range(1, len(pairs)):
        loads["fac", p].start()
    loaded = set()

    def need(*key):
        if key not in loaded:
            loads[key].wait()
            loaded.add(key)

    sends = []

    def send(phase, h, slot, src, dst, device):
        copy = pltpu.make_async_remote_copy(
            src_ref=src,
            dst_ref=dst,
            send_sem=send_sem.at[phase, h, slot],
            recv_sem=recv_sem.at[phase, h, slot],
            device_id=device,
            device_id_type=MESH,
        )
        copy.start()
        sends.append(copy)
        return copy

    def dot_t(a, b):
        return lax.dot_general(a, b, (((1,), (1,)), ((), ())), preferred_element_type=jnp.float32)

    def dot_n(a, b):
        return jnp.dot(a, b, preferred_element_type=jnp.float32)

    def order(vals):
        return [k for k in (2, 3, 1) if k < len(vals)] + list(range(4, len(vals)))

    def product(p, panels, table, width, dot):
        need("fac", p)
        total = None
        for q in range(slots):
            picks = [ref[table[p, q, j]] for ref in panels for j in range(width)]
            term = dot(jnp.concatenate(picks, axis=0), fac[p, q])
            total = term if total is None else total + term
        return total

    def spread(phase, h, vals, device, total, part, recv):
        copies = []
        for k in order(vals):
            part[k] = total[k * rows : (k + 1) * rows].astype(jnp.bfloat16)
            copies.append(send(phase, h, k, part.at[k], recv.at[k], device(vals[k])))
        return copies, total[:rows].astype(jnp.bfloat16).astype(jnp.float32)

    def collect(copies, recv, own, width):
        for copy in copies:
            copy.wait_recv()
        for k in range(1, width):
            own = own + recv[k].astype(jnp.float32)
        return own

    def share(phase, h, vals, device, panels):
        return [
            send(phase, h, k, panels.at[0], panels.at[k], device(-vals[k])) for k in order(vals)
        ]

    everyone = range(streams)

    def part_of(h):
        return pl.ds(h * rows, rows)

    need("rhs", 0)
    need("inv", 0)
    y = dot_t(rhs[0].astype(jnp.bfloat16), inv[0])
    yfull[0] = y
    for h in everyone:
        ycol[h][0][0] = y[h * rows : (h + 1) * rows].astype(jnp.bfloat16)
    pl.semaphore_wait(barrier, row_w + col_w - 2)
    phase = 0
    copies = [share(phase, h, col_vals, col_dev, ycol[h][0]) for h in everyone]

    zero = jnp.zeros((rows, rhs.shape[2]), jnp.bfloat16)
    for h in everyone:
        for lvl in range(levels - 1):
            ycol[h][lvl][col_w] = zero
            brow[h][lvl + 1][row_w] = zero
    need("tgt", 0)
    need("src", 0)
    for p in range(len(pairs)):
        for q in range(slots):
            off_r = tgt_ref[p, 0, q] - me_r
            off_c = src_ref[p, 0, q] - me_c
            off_r = jnp.where(off_r < 0, off_r + n_row, off_r)
            off_c = jnp.where(off_c < 0, off_c + n_col, off_c)
            pos_r = jnp.int32(0)
            for k in range(1, row_w):
                pos_r = jnp.where(off_r == row_vals[k], k, pos_r)
            pos_c = jnp.int32(0)
            for k in range(1, col_w):
                pos_c = jnp.where(off_c == col_vals[k], k, pos_c)
            for k in range(row_w):
                ftab[p, q, k] = jnp.where(pos_r == k, pos_c, col_w)
            for k in range(col_w):
                btab[p, q, k] = jnp.where(pos_c == k, pos_r, row_w)

    for k in range(1, levels):
        near = pairs.index((k, k - 1))
        own = [None] * streams
        for h in everyone:
            for copy in copies[h]:
                copy.wait_recv()
            total = product(near, [ycol[h][k - 1]], ftab, row_w, dot_t)
            if k > 1:
                total = total + facc[k, pl.ds(h * row_w * rows, row_w * rows)]
            copies[h], own[h] = spread(
                phase + 1, h, row_vals, row_dev, total, fpart.at[h, k], frecv.at[h, k]
            )
        for p, (d, s) in enumerate(pairs):
            if s == k - 1 and d > k:
                later = product(p, [ycol[h][s] for h in everyone], ftab, row_w, dot_t)
                facc[d] = later if s == 0 else facc[d] + later
        need("rhs", k)
        need("inv", k)
        answers = [None] * streams
        for h in everyone:
            fsum = collect(copies[h], frecv.at[h, k], own[h], row_w)
            y = dot_t((rhs[k, part_of(h)] - fsum).astype(jnp.bfloat16), inv[k])
            ybf = y.astype(jnp.bfloat16)
            if k < levels - 1:
                ycol[h][k][0] = ybf
                copies[h] = share(phase + 2, h, col_vals, col_dev, ycol[h][k])
                yfull[k, part_of(h)] = y
            else:
                answers[h] = dot_n(ybf, inv[k])
                brow[h][k][0] = answers[h].astype(jnp.bfloat16)
                copies[h] = share(phase + 2, h, row_vals, row_dev, brow[h][k])
                out_ref[k, 0, 0, part_of(h)] = answers[h]
        phase += 2

    top = levels - 1
    for k in reversed(range(top)):
        near = pairs.index((k + 1, k))
        own = [None] * streams
        for h in everyone:
            for copy in copies[h]:
                copy.wait_recv()
            total = product(near, [brow[h][k + 1]], btab, col_w, dot_n)
            if k + 1 < top:
                total = total + bacc[k, pl.ds(h * col_w * rows, col_w * rows)]
            copies[h], own[h] = spread(
                phase + 1, h, col_vals, col_dev, total, bpart.at[h, k], brecv.at[h, k]
            )
        for p, (d, s) in enumerate(pairs):
            if d == k + 1 and s < k:
                later = product(p, [brow[h][d] for h in everyone], btab, col_w, dot_n)
                bacc[s] = later if d == top else bacc[s] + later
        for h in everyone:
            bsum = collect(copies[h], brecv.at[h, k], own[h], col_w)
            answer = dot_n((yfull[k, part_of(h)] - bsum).astype(jnp.bfloat16), inv[k])
            if k > 0:
                brow[h][k][0] = answer.astype(jnp.bfloat16)
                copies[h] = share(phase + 2, h, row_vals, row_dev, brow[h][k])
            out_ref[k, 0, 0, part_of(h)] = answer
        phase += 2
    for copy in sends:
        copy.wait_send()


def shards(n_row, n_col, rhs, inv, fac, tgt, src):
    levels, nrhs, size = rhs.shape[0], rhs.shape[3], rhs.shape[4]
    pairs, slots = fac.shape[0], fac.shape[2]
    row_w = len(offset_choices(WINDOW, n_row))
    col_w = len(offset_choices(WINDOW, n_col))
    width = max(row_w, col_w)
    phases = 4 * (levels - 1)
    rows = nrhs // STREAMS
    bf, f32 = jnp.bfloat16, jnp.float32
    return pl.pallas_call(
        functools.partial(kernel, n_row, n_col),
        out_shape=pltpu.VMEM(rhs.shape, f32),
        in_specs=[pl.BlockSpec(memory_space=pl.ANY)] * 5,
        out_specs=pl.BlockSpec(memory_space=pltpu.VMEM),
        scratch_shapes=[
            pltpu.VMEM((levels, nrhs, size), f32),
            pltpu.VMEM((levels, size, size), bf),
            pltpu.VMEM((pairs, slots, size, size), bf),
            [[pltpu.VMEM((col_w + 1, rows, size), bf)] * (levels - 1)] * STREAMS,
            [[pltpu.VMEM((row_w + 1, rows, size), bf)] * levels] * STREAMS,
            pltpu.VMEM((STREAMS, levels, row_w, rows, size), bf),
            pltpu.VMEM((STREAMS, levels, row_w, rows, size), bf),
            pltpu.VMEM((STREAMS, levels - 1, col_w, rows, size), bf),
            pltpu.VMEM((STREAMS, levels - 1, col_w, rows, size), bf),
            pltpu.VMEM((levels - 1, nrhs, size), f32),
            pltpu.VMEM((levels, row_w * nrhs, size), f32),
            pltpu.VMEM((levels - 1, col_w * nrhs, size), f32),
            pltpu.SMEM(tgt.shape, jnp.int32),
            pltpu.SMEM(src.shape, jnp.int32),
            pltpu.SMEM((pairs, slots, row_w), jnp.int32),
            pltpu.SMEM((pairs, slots, col_w), jnp.int32),
            pltpu.SemaphoreType.DMA((2,)),
            pltpu.SemaphoreType.DMA((levels,)),
            pltpu.SemaphoreType.DMA((levels,)),
            pltpu.SemaphoreType.DMA((pairs,)),
            pltpu.SemaphoreType.DMA((phases, STREAMS, width)),
            pltpu.SemaphoreType.DMA((phases, STREAMS, width)),
        ],
        compiler_params=pltpu.CompilerParams(collective_id=0, has_side_effects=True),
    )(rhs, inv, fac, tgt, src)


def solution(mesh):
    placed = (
        P(None, "row", "col", None, None),
        P(None, "row", "col", None, None),
        P(None, "row", "col", None, None),
        P(None, "row", "col"),
        P(None, "row", "col"),
    )
    return jax.shard_map(
        functools.partial(shards, mesh.shape["row"], mesh.shape["col"]),
        mesh=mesh,
        in_specs=placed,
        out_specs=P(None, "row", "col", None, None),
        check_vma=False,
    )
```

```python
import functools

import jax
import jax.numpy as jnp
from jax import lax
from jax.experimental import pallas as pl
from jax.experimental.pallas import tpu as pltpu
from jax.sharding import PartitionSpec as P

WINDOW = 2
STREAMS = 2
MESH = pl.DeviceIdType.MESH


def pair_table(levels):
    return [(d, s) for d in range(1, levels) for s in range(d)]


def offset_choices(window, count):
    return sorted(set(list(range(window)) + [count // 2, count - 1]))


def kernel(
    n_row,
    n_col,
    rhs_hbm,
    inv_hbm,
    fac_hbm,
    tgt_hbm,
    src_hbm,
    out_ref,
    rhs,
    inv,
    fac,
    ycol,
    brow,
    fpart,
    frecv,
    bpart,
    brecv,
    yfull,
    facc,
    bacc,
    tgt_ref,
    src_ref,
    ftab,
    btab,
    idx_sem,
    rhs_sem,
    inv_sem,
    fac_sem,
    send_sem,
    recv_sem,
):
    levels = rhs.shape[0]
    slots = fac.shape[1]
    streams = len(ycol)
    rows = rhs.shape[1] // streams
    pairs = pair_table(levels)
    row_vals = offset_choices(WINDOW, n_row)
    col_vals = offset_choices(WINDOW, n_col)
    row_w, col_w = len(row_vals), len(col_vals)
    me_r, me_c = lax.axis_index("row"), lax.axis_index("col")

    def row_dev(steps):
        return {"row": lax.rem(me_r + (steps + n_row), n_row)}

    def col_dev(steps):
        return {"col": lax.rem(me_c + (steps + n_col), n_col)}

    barrier = pltpu.get_barrier_semaphore()
    for v in row_vals[1:]:
        pl.semaphore_signal(barrier, inc=1, device_id=row_dev(v), device_id_type=MESH)
    for v in col_vals[1:]:
        pl.semaphore_signal(barrier, inc=1, device_id=col_dev(v), device_id_type=MESH)

    loads = {}
    for k in range(levels):
        loads["rhs", k] = pltpu.make_async_copy(rhs_hbm.at[k, 0, 0], rhs.at[k], rhs_sem.at[k])
        loads["inv", k] = pltpu.make_async_copy(inv_hbm.at[k, 0, 0], inv.at[k], inv_sem.at[k])
    for p in range(len(pairs)):
        loads["fac", p] = pltpu.make_async_copy(fac_hbm.at[p, 0], fac.at[p], fac_sem.at[p])
    loads["rhs", 0].start()
    loads["inv", 0].start()
    loads["tgt", 0] = pltpu.make_async_copy(tgt_hbm, tgt_ref, idx_sem.at[0])
    loads["src", 0] = pltpu.make_async_copy(src_hbm, src_ref, idx_sem.at[1])
    loads["tgt", 0].start()
    loads["src", 0].start()
    loads["fac", 0].start()
    for k in range(1, levels):
        loads["rhs", k].start()
        loads["inv", k].start()
    for p in range(1, len(pairs)):
        loads["fac", p].start()
    loaded = set()

    def need(*key):
        if key not in loaded:
            loads[key].wait()
            loaded.add(key)

    def send(phase, h, src, dst, device):
        pltpu.make_async_remote_copy(
            src_ref=src,
            dst_ref=dst,
            send_sem=send_sem.at[0],
            recv_sem=recv_sem.at[phase, h],
            device_id=device,
            device_id_type=MESH,
        ).start()

    def arrive(phase, h, landed, width):
        slabs = landed.at[pl.ds(1, width - 1)]
        pltpu.make_async_copy(slabs, slabs, recv_sem.at[phase, h]).wait()

    def dot_t(a, b):
        return lax.dot_general(a, b, (((1,), (1,)), ((), ())), preferred_element_type=jnp.float32)

    def dot_n(a, b):
        return jnp.dot(a, b, preferred_element_type=jnp.float32)

    def order(vals):
        return [k for k in (2, 3, 1) if k < len(vals)] + list(range(4, len(vals)))

    def product(p, panels, table, width, dot):
        need("fac", p)
        total = None
        for q in range(slots):
            picks = [ref[table[p, q, j]] for ref in panels for j in range(width)]
            term = dot(jnp.concatenate(picks, axis=0), fac[p, q])
            total = term if total is None else total + term
        return total

    def spread(phase, h, vals, device, total, part, recv):
        for k in order(vals):
            part[k] = total[k * rows : (k + 1) * rows].astype(jnp.bfloat16)
            send(phase, h, part.at[k], recv.at[k], device(vals[k]))
        return total[:rows].astype(jnp.bfloat16).astype(jnp.float32)

    def collect(phase, h, recv, own, width):
        arrive(phase, h, recv, width)
        for k in range(1, width):
            own = own + recv[k].astype(jnp.float32)
        return own

    def share(phase, h, vals, device, panels):
        for k in order(vals):
            send(phase, h, panels.at[0], panels.at[k], device(-vals[k]))

    everyone = range(streams)

    def part_of(h):
        return pl.ds(h * rows, rows)

    need("rhs", 0)
    need("inv", 0)
    y = dot_t(rhs[0].astype(jnp.bfloat16), inv[0])
    yfull[0] = y
    for h in everyone:
        ycol[h][0][0] = y[h * rows : (h + 1) * rows].astype(jnp.bfloat16)
    pl.semaphore_wait(barrier, row_w + col_w - 2)
    phase = 0
    for h in everyone:
        share(phase, h, col_vals, col_dev, ycol[h][0])

    zero = jnp.zeros((rows, rhs.shape[2]), jnp.bfloat16)
    for h in everyone:
        for lvl in range(levels - 1):
            ycol[h][lvl][col_w] = zero
            brow[h][lvl + 1][row_w] = zero
    need("tgt", 0)
    need("src", 0)
    for p in range(len(pairs)):
        for q in range(slots):
            off_r = tgt_ref[p, 0, q] - me_r
            off_c = src_ref[p, 0, q] - me_c
            off_r = jnp.where(off_r < 0, off_r + n_row, off_r)
            off_c = jnp.where(off_c < 0, off_c + n_col, off_c)
            pos_r = jnp.int32(0)
            for k in range(1, row_w):
                pos_r = jnp.where(off_r == row_vals[k], k, pos_r)
            pos_c = jnp.int32(0)
            for k in range(1, col_w):
                pos_c = jnp.where(off_c == col_vals[k], k, pos_c)
            for k in range(row_w):
                ftab[p, q, k] = jnp.where(pos_r == k, pos_c, col_w)
            for k in range(col_w):
                btab[p, q, k] = jnp.where(pos_c == k, pos_r, row_w)

    for k in range(1, levels):
        near = pairs.index((k, k - 1))
        own = [None] * streams
        for h in everyone:
            arrive(phase, h, ycol[h][k - 1], col_w)
            total = product(near, [ycol[h][k - 1]], ftab, row_w, dot_t)
            if k > 1:
                total = total + facc[k, pl.ds(h * row_w * rows, row_w * rows)]
            own[h] = spread(
                phase + 1, h, row_vals, row_dev, total, fpart.at[h, k], frecv.at[h, k]
            )
        for p, (d, s) in enumerate(pairs):
            if s == k - 1 and d > k:
                later = product(p, [ycol[h][s] for h in everyone], ftab, row_w, dot_t)
                facc[d] = later if s == 0 else facc[d] + later
        need("rhs", k)
        need("inv", k)
        answers = [None] * streams
        for h in everyone:
            fsum = collect(phase + 1, h, frecv.at[h, k], own[h], row_w)
            y = dot_t((rhs[k, part_of(h)] - fsum).astype(jnp.bfloat16), inv[k])
            ybf = y.astype(jnp.bfloat16)
            if k < levels - 1:
                ycol[h][k][0] = ybf
                share(phase + 2, h, col_vals, col_dev, ycol[h][k])
                yfull[k, part_of(h)] = y
            else:
                answers[h] = dot_n(ybf, inv[k])
                brow[h][k][0] = answers[h].astype(jnp.bfloat16)
                share(phase + 2, h, row_vals, row_dev, brow[h][k])
                out_ref[k, 0, 0, part_of(h)] = answers[h]
        phase += 2

    top = levels - 1
    for k in reversed(range(top)):
        near = pairs.index((k + 1, k))
        own = [None] * streams
        for h in everyone:
            arrive(phase, h, brow[h][k + 1], row_w)
            total = product(near, [brow[h][k + 1]], btab, col_w, dot_n)
            if k + 1 < top:
                total = total + bacc[k, pl.ds(h * col_w * rows, col_w * rows)]
            own[h] = spread(
                phase + 1, h, col_vals, col_dev, total, bpart.at[h, k], brecv.at[h, k]
            )
        for p, (d, s) in enumerate(pairs):
            if d == k + 1 and s < k:
                later = product(p, [brow[h][d] for h in everyone], btab, col_w, dot_n)
                bacc[s] = later if d == top else bacc[s] + later
        for h in everyone:
            bsum = collect(phase + 1, h, brecv.at[h, k], own[h], col_w)
            answer = dot_n((yfull[k, part_of(h)] - bsum).astype(jnp.bfloat16), inv[k])
            if k > 0:
                brow[h][k][0] = answer.astype(jnp.bfloat16)
                share(phase + 2, h, row_vals, row_dev, brow[h][k])
            out_ref[k, 0, 0, part_of(h)] = answer
        phase += 2
    panels_sent = (levels - 1) * 2 * (row_w + col_w - 2)
    sent = fac.at[0, pl.ds(0, panels_sent * rhs.shape[1] // fac.shape[2])]
    pltpu.make_async_copy(sent, sent, send_sem.at[0]).wait()


def shards(n_row, n_col, rhs, inv, fac, tgt, src):
    levels, nrhs, size = rhs.shape[0], rhs.shape[3], rhs.shape[4]
    pairs, slots = fac.shape[0], fac.shape[2]
    row_w = len(offset_choices(WINDOW, n_row))
    col_w = len(offset_choices(WINDOW, n_col))
    phases = 4 * (levels - 1)
    rows = nrhs // STREAMS
    bf, f32 = jnp.bfloat16, jnp.float32
    return pl.pallas_call(
        functools.partial(kernel, n_row, n_col),
        out_shape=pltpu.VMEM(rhs.shape, f32),
        in_specs=[pl.BlockSpec(memory_space=pl.ANY)] * 5,
        out_specs=pl.BlockSpec(memory_space=pltpu.VMEM),
        scratch_shapes=[
            pltpu.VMEM((levels, nrhs, size), f32),
            pltpu.VMEM((levels, size, size), bf),
            pltpu.VMEM((pairs, slots, size, size), bf),
            [[pltpu.VMEM((col_w + 1, rows, size), bf)] * (levels - 1)] * STREAMS,
            [[pltpu.VMEM((row_w + 1, rows, size), bf)] * levels] * STREAMS,
            pltpu.VMEM((STREAMS, levels, row_w, rows, size), bf),
            pltpu.VMEM((STREAMS, levels, row_w, rows, size), bf),
            pltpu.VMEM((STREAMS, levels - 1, col_w, rows, size), bf),
            pltpu.VMEM((STREAMS, levels - 1, col_w, rows, size), bf),
            pltpu.VMEM((levels - 1, nrhs, size), f32),
            pltpu.VMEM((levels, row_w * nrhs, size), f32),
            pltpu.VMEM((levels - 1, col_w * nrhs, size), f32),
            pltpu.SMEM(tgt.shape, jnp.int32),
            pltpu.SMEM(src.shape, jnp.int32),
            pltpu.SMEM((pairs, slots, row_w), jnp.int32),
            pltpu.SMEM((pairs, slots, col_w), jnp.int32),
            pltpu.SemaphoreType.DMA((2,)),
            pltpu.SemaphoreType.DMA((levels,)),
            pltpu.SemaphoreType.DMA((levels,)),
            pltpu.SemaphoreType.DMA((pairs,)),
            pltpu.SemaphoreType.DMA((1,)),
            pltpu.SemaphoreType.DMA((phases, STREAMS)),
        ],
        compiler_params=pltpu.CompilerParams(collective_id=0, has_side_effects=True),
    )(rhs, inv, fac, tgt, src)


def solution(mesh):
    placed = (
        P(None, "row", "col", None, None),
        P(None, "row", "col", None, None),
        P(None, "row", "col", None, None),
        P(None, "row", "col"),
        P(None, "row", "col"),
    )
    return jax.shard_map(
        functools.partial(shards, mesh.shape["row"], mesh.shape["col"]),
        mesh=mesh,
        in_specs=placed,
        out_specs=P(None, "row", "col", None, None),
        check_vma=False,
    )
```

```python
import functools

import jax
import jax.numpy as jnp
from jax import lax
from jax.experimental import pallas as pl
from jax.experimental.pallas import tpu as pltpu
from jax.sharding import PartitionSpec as P

WINDOW = 2
STREAMS = 2
MESH = pl.DeviceIdType.MESH


def pair_table(levels):
    return [(d, s) for d in range(1, levels) for s in range(d)]


def offset_choices(window, count):
    return sorted(set(list(range(window)) + [count // 2, count - 1]))


def kernel(
    n_row,
    n_col,
    rhs_hbm,
    inv_hbm,
    fac_hbm,
    tgt_hbm,
    src_hbm,
    out_ref,
    rhs,
    inv,
    fac,
    ycol,
    brow,
    fpart,
    frecv,
    bpart,
    brecv,
    yfull,
    facc,
    bacc,
    tgt_ref,
    src_ref,
    ftab,
    btab,
    idx_sem,
    rhs_sem,
    inv_sem,
    fac_sem,
    send_sem,
    recv_sem,
):
    levels = rhs.shape[0]
    slots = fac.shape[1]
    streams = len(ycol)
    rows = rhs.shape[1] // streams
    pairs = pair_table(levels)
    row_vals = offset_choices(WINDOW, n_row)
    col_vals = offset_choices(WINDOW, n_col)
    row_w, col_w = len(row_vals), len(col_vals)
    me_r, me_c = lax.axis_index("row"), lax.axis_index("col")

    def row_dev(steps):
        return {"row": lax.rem(me_r + (steps + n_row), n_row)}

    def col_dev(steps):
        return {"col": lax.rem(me_c + (steps + n_col), n_col)}

    barrier = pltpu.get_barrier_semaphore()
    for v in row_vals[1:]:
        pl.semaphore_signal(barrier, inc=1, device_id=row_dev(v), device_id_type=MESH)
    for v in col_vals[1:]:
        pl.semaphore_signal(barrier, inc=1, device_id=col_dev(v), device_id_type=MESH)

    loads = {}
    for k in range(levels):
        loads["rhs", k] = pltpu.make_async_copy(rhs_hbm.at[k, 0, 0], rhs.at[k], rhs_sem.at[k])
        loads["inv", k] = pltpu.make_async_copy(inv_hbm.at[k, 0, 0], inv.at[k], inv_sem.at[k])
    for p in range(len(pairs)):
        loads["fac", p] = pltpu.make_async_copy(fac_hbm.at[p, 0], fac.at[p], fac_sem.at[p])
    loads["rhs", 0].start()
    loads["inv", 0].start()
    loads["tgt", 0] = pltpu.make_async_copy(tgt_hbm, tgt_ref, idx_sem.at[0])
    loads["src", 0] = pltpu.make_async_copy(src_hbm, src_ref, idx_sem.at[1])
    loads["tgt", 0].start()
    loads["src", 0].start()
    loads["fac", 0].start()
    for k in range(1, levels):
        loads["rhs", k].start()
        loads["inv", k].start()
    for p in range(1, len(pairs)):
        loads["fac", p].start()
    loaded = set()

    def need(*key):
        if key not in loaded:
            loads[key].wait()
            loaded.add(key)

    def send(phase, h, src, dst, device):
        pltpu.make_async_remote_copy(
            src_ref=src,
            dst_ref=dst,
            send_sem=send_sem.at[0],
            recv_sem=recv_sem.at[phase, h],
            device_id=device,
            device_id_type=MESH,
        ).start()

    def arrive(phase, h, landed, width):
        slabs = landed.at[pl.ds(1, width - 1)]
        pltpu.make_async_copy(slabs, slabs, recv_sem.at[phase, h]).wait()

    def dot_t(a, b):
        return lax.dot_general(a, b, (((1,), (1,)), ((), ())), preferred_element_type=jnp.float32)

    def dot_n(a, b):
        return jnp.dot(a, b, preferred_element_type=jnp.float32)

    def order(vals):
        return [k for k in (2, 3, 1) if k < len(vals)] + list(range(4, len(vals)))

    def product(p, panels, table, width, dot):
        need("fac", p)
        total = None
        for q in range(slots):
            picks = [ref[table[p, q, j]] for ref in panels for j in range(width)]
            term = dot(jnp.concatenate(picks, axis=0), fac[p, q])
            total = term if total is None else total + term
        return total

    def turns(vals, me, count, sign):
        slots_left = list(range(1, len(vals)))
        far = []
        for k in slots_left:
            peer = lax.rem(me + (sign * vals[k] + count), count)
            far.append(jnp.abs(peer - me))
        ranks = []
        for i, k in enumerate(slots_left):
            rank = jnp.int32(0)
            for j in range(len(slots_left)):
                if j < i:
                    rank = rank + jnp.where(far[j] >= far[i], 1, 0)
                elif j > i:
                    rank = rank + jnp.where(far[j] > far[i], 1, 0)
            ranks.append(rank)
        picked = []
        for turn in range(len(slots_left)):
            k_now, v_now = jnp.int32(0), jnp.int32(0)
            for i, k in enumerate(slots_left):
                k_now = jnp.where(ranks[i] == turn, k, k_now)
                v_now = jnp.where(ranks[i] == turn, vals[k], v_now)
            picked.append((k_now, v_now))
        return picked

    row_out = turns(row_vals, me_r, n_row, 1)
    row_back = turns(row_vals, me_r, n_row, -1)

    def spread(phase, h, vals, device, total, part, recv):
        for k in order(vals):
            part[k] = total[k * rows : (k + 1) * rows].astype(jnp.bfloat16)
            if device is col_dev:
                send(phase, h, part.at[k], recv.at[k], device(vals[k]))
        if device is row_dev:
            for k, v in row_out:
                send(phase, h, part.at[k], recv.at[k], device(v))
        return total[:rows].astype(jnp.bfloat16).astype(jnp.float32)

    def collect(phase, h, recv, own, width):
        arrive(phase, h, recv, width)
        for k in range(1, width):
            own = own + recv[k].astype(jnp.float32)
        return own

    def share(phase, h, vals, device, panels):
        if device is row_dev:
            for k, v in row_back:
                send(phase, h, panels.at[0], panels.at[k], device(-v))
        else:
            for k in order(vals):
                send(phase, h, panels.at[0], panels.at[k], device(-vals[k]))

    everyone = range(streams)

    def part_of(h):
        return pl.ds(h * rows, rows)

    need("rhs", 0)
    need("inv", 0)
    y = dot_t(rhs[0].astype(jnp.bfloat16), inv[0])
    yfull[0] = y
    for h in everyone:
        ycol[h][0][0] = y[h * rows : (h + 1) * rows].astype(jnp.bfloat16)
    pl.semaphore_wait(barrier, row_w + col_w - 2)
    phase = 0
    for h in everyone:
        share(phase, h, col_vals, col_dev, ycol[h][0])

    zero = jnp.zeros((rows, rhs.shape[2]), jnp.bfloat16)
    for h in everyone:
        for lvl in range(levels - 1):
            ycol[h][lvl][col_w] = zero
            brow[h][lvl + 1][row_w] = zero
    need("tgt", 0)
    need("src", 0)
    for p in range(len(pairs)):
        for q in range(slots):
            off_r = tgt_ref[p, 0, q] - me_r
            off_c = src_ref[p, 0, q] - me_c
            off_r = jnp.where(off_r < 0, off_r + n_row, off_r)
            off_c = jnp.where(off_c < 0, off_c + n_col, off_c)
            pos_r = jnp.int32(0)
            for k in range(1, row_w):
                pos_r = jnp.where(off_r == row_vals[k], k, pos_r)
            pos_c = jnp.int32(0)
            for k in range(1, col_w):
                pos_c = jnp.where(off_c == col_vals[k], k, pos_c)
            for k in range(row_w):
                ftab[p, q, k] = jnp.where(pos_r == k, pos_c, col_w)
            for k in range(col_w):
                btab[p, q, k] = jnp.where(pos_c == k, pos_r, row_w)

    for k in range(1, levels):
        near = pairs.index((k, k - 1))
        own = [None] * streams
        for h in everyone:
            arrive(phase, h, ycol[h][k - 1], col_w)
            total = product(near, [ycol[h][k - 1]], ftab, row_w, dot_t)
            if k > 1:
                total = total + facc[k, pl.ds(h * row_w * rows, row_w * rows)]
            own[h] = spread(
                phase + 1, h, row_vals, row_dev, total, fpart.at[h, k], frecv.at[h, k]
            )
        for p, (d, s) in enumerate(pairs):
            if s == k - 1 and d > k:
                later = product(p, [ycol[h][s] for h in everyone], ftab, row_w, dot_t)
                facc[d] = later if s == 0 else facc[d] + later
        need("rhs", k)
        need("inv", k)
        answers = [None] * streams
        for h in everyone:
            fsum = collect(phase + 1, h, frecv.at[h, k], own[h], row_w)
            y = dot_t((rhs[k, part_of(h)] - fsum).astype(jnp.bfloat16), inv[k])
            ybf = y.astype(jnp.bfloat16)
            if k < levels - 1:
                ycol[h][k][0] = ybf
                share(phase + 2, h, col_vals, col_dev, ycol[h][k])
                yfull[k, part_of(h)] = y
            else:
                answers[h] = dot_n(ybf, inv[k])
                brow[h][k][0] = answers[h].astype(jnp.bfloat16)
                share(phase + 2, h, row_vals, row_dev, brow[h][k])
                out_ref[k, 0, 0, part_of(h)] = answers[h]
        phase += 2

    top = levels - 1
    for k in reversed(range(top)):
        near = pairs.index((k + 1, k))
        own = [None] * streams
        for h in everyone:
            arrive(phase, h, brow[h][k + 1], row_w)
            total = product(near, [brow[h][k + 1]], btab, col_w, dot_n)
            if k + 1 < top:
                total = total + bacc[k, pl.ds(h * col_w * rows, col_w * rows)]
            own[h] = spread(
                phase + 1, h, col_vals, col_dev, total, bpart.at[h, k], brecv.at[h, k]
            )
        for p, (d, s) in enumerate(pairs):
            if d == k + 1 and s < k:
                later = product(p, [brow[h][d] for h in everyone], btab, col_w, dot_n)
                bacc[s] = later if d == top else bacc[s] + later
        for h in everyone:
            bsum = collect(phase + 1, h, brecv.at[h, k], own[h], col_w)
            answer = dot_n((yfull[k, part_of(h)] - bsum).astype(jnp.bfloat16), inv[k])
            if k > 0:
                brow[h][k][0] = answer.astype(jnp.bfloat16)
                share(phase + 2, h, row_vals, row_dev, brow[h][k])
            out_ref[k, 0, 0, part_of(h)] = answer
        phase += 2
    panels_sent = (levels - 1) * 2 * (row_w + col_w - 2)
    sent = fac.at[0, pl.ds(0, panels_sent * rhs.shape[1] // fac.shape[2])]
    pltpu.make_async_copy(sent, sent, send_sem.at[0]).wait()


def shards(n_row, n_col, rhs, inv, fac, tgt, src):
    levels, nrhs, size = rhs.shape[0], rhs.shape[3], rhs.shape[4]
    pairs, slots = fac.shape[0], fac.shape[2]
    row_w = len(offset_choices(WINDOW, n_row))
    col_w = len(offset_choices(WINDOW, n_col))
    phases = 4 * (levels - 1)
    rows = nrhs // STREAMS
    bf, f32 = jnp.bfloat16, jnp.float32
    return pl.pallas_call(
        functools.partial(kernel, n_row, n_col),
        out_shape=pltpu.VMEM(rhs.shape, f32),
        in_specs=[pl.BlockSpec(memory_space=pl.ANY)] * 5,
        out_specs=pl.BlockSpec(memory_space=pltpu.VMEM),
        scratch_shapes=[
            pltpu.VMEM((levels, nrhs, size), f32),
            pltpu.VMEM((levels, size, size), bf),
            pltpu.VMEM((pairs, slots, size, size), bf),
            [[pltpu.VMEM((col_w + 1, rows, size), bf)] * (levels - 1)] * STREAMS,
            [[pltpu.VMEM((row_w + 1, rows, size), bf)] * levels] * STREAMS,
            pltpu.VMEM((STREAMS, levels, row_w, rows, size), bf),
            pltpu.VMEM((STREAMS, levels, row_w, rows, size), bf),
            pltpu.VMEM((STREAMS, levels - 1, col_w, rows, size), bf),
            pltpu.VMEM((STREAMS, levels - 1, col_w, rows, size), bf),
            pltpu.VMEM((levels - 1, nrhs, size), f32),
            pltpu.VMEM((levels, row_w * nrhs, size), f32),
            pltpu.VMEM((levels - 1, col_w * nrhs, size), f32),
            pltpu.SMEM(tgt.shape, jnp.int32),
            pltpu.SMEM(src.shape, jnp.int32),
            pltpu.SMEM((pairs, slots, row_w), jnp.int32),
            pltpu.SMEM((pairs, slots, col_w), jnp.int32),
            pltpu.SemaphoreType.DMA((2,)),
            pltpu.SemaphoreType.DMA((levels,)),
            pltpu.SemaphoreType.DMA((levels,)),
            pltpu.SemaphoreType.DMA((pairs,)),
            pltpu.SemaphoreType.DMA((1,)),
            pltpu.SemaphoreType.DMA((phases, STREAMS)),
        ],
        compiler_params=pltpu.CompilerParams(collective_id=0, has_side_effects=True),
    )(rhs, inv, fac, tgt, src)


def solution(mesh):
    placed = (
        P(None, "row", "col", None, None),
        P(None, "row", "col", None, None),
        P(None, "row", "col", None, None),
        P(None, "row", "col"),
        P(None, "row", "col"),
    )
    return jax.shard_map(
        functools.partial(shards, mesh.shape["row"], mesh.shape["col"]),
        mesh=mesh,
        in_specs=placed,
        out_specs=P(None, "row", "col", None, None),
        check_vma=False,
    )
```

```python
import functools

import jax
import jax.numpy as jnp
from jax import lax
from jax.experimental import pallas as pl
from jax.experimental.pallas import tpu as pltpu
from jax.sharding import PartitionSpec as P

WINDOW = 2
STREAMS = 2
MESH = pl.DeviceIdType.MESH


def pair_table(levels):
    return [(d, s) for d in range(1, levels) for s in range(d)]


def offset_choices(window, count):
    return sorted(set(list(range(window)) + [count // 2, count - 1]))


def kernel(
    n_row,
    n_col,
    rhs_hbm,
    inv_hbm,
    fac_hbm,
    tgt_hbm,
    src_hbm,
    out_ref,
    rhs,
    inv,
    fac,
    ycol,
    brow,
    fpart,
    frecv,
    bpart,
    brecv,
    yfull,
    facc,
    bacc,
    tgt_ref,
    src_ref,
    ftab,
    btab,
    idx_sem,
    rhs_sem,
    inv_sem,
    fac_sem,
    send_sem,
    recv_sem,
):
    levels = rhs.shape[0]
    slots = fac.shape[1]
    streams = len(ycol)
    rows = rhs.shape[1] // streams
    pairs = pair_table(levels)
    row_vals = offset_choices(WINDOW, n_row)
    col_vals = offset_choices(WINDOW, n_col)
    row_w, col_w = len(row_vals), len(col_vals)
    me_r, me_c = lax.axis_index("row"), lax.axis_index("col")

    def row_dev(steps):
        return {"row": lax.rem(me_r + (steps + n_row), n_row)}

    def col_dev(steps):
        return {"col": lax.rem(me_c + (steps + n_col), n_col)}

    loads = {}
    for k in range(levels):
        loads["rhs", k] = pltpu.make_async_copy(rhs_hbm.at[k, 0, 0], rhs.at[k], rhs_sem.at[k])
        loads["inv", k] = pltpu.make_async_copy(inv_hbm.at[k, 0, 0], inv.at[k], inv_sem.at[k])
    for p in range(len(pairs)):
        loads["fac", p] = pltpu.make_async_copy(fac_hbm.at[p, 0], fac.at[p], fac_sem.at[p])
    loads["rhs", 0].start()
    loads["inv", 0].start()
    barrier = pltpu.get_barrier_semaphore()
    for v in row_vals[1:]:
        pl.semaphore_signal(barrier, inc=1, device_id=row_dev(v), device_id_type=MESH)
    for v in col_vals[1:]:
        pl.semaphore_signal(barrier, inc=1, device_id=col_dev(v), device_id_type=MESH)

    loads["tgt", 0] = pltpu.make_async_copy(tgt_hbm, tgt_ref, idx_sem.at[0])
    loads["src", 0] = pltpu.make_async_copy(src_hbm, src_ref, idx_sem.at[1])
    loads["tgt", 0].start()
    loads["src", 0].start()
    loads["fac", 0].start()
    for k in range(1, levels):
        loads["rhs", k].start()
        loads["inv", k].start()
    for p in range(1, len(pairs)):
        loads["fac", p].start()
    loaded = set()

    def need(*key):
        if key not in loaded:
            loads[key].wait()
            loaded.add(key)

    def send(phase, h, src, dst, device):
        pltpu.make_async_remote_copy(
            src_ref=src,
            dst_ref=dst,
            send_sem=send_sem.at[0],
            recv_sem=recv_sem.at[phase, h],
            device_id=device,
            device_id_type=MESH,
        ).start()

    def arrive(phase, h, landed, width):
        slabs = landed.at[pl.ds(1, width - 1)]
        pltpu.make_async_copy(slabs, slabs, recv_sem.at[phase, h]).wait()

    def dot_t(a, b):
        return lax.dot_general(a, b, (((1,), (1,)), ((), ())), preferred_element_type=jnp.float32)

    def dot_n(a, b):
        return jnp.dot(a, b, preferred_element_type=jnp.float32)

    def order(vals):
        return [k for k in (2, 3, 1) if k < len(vals)] + list(range(4, len(vals)))

    def product(p, panels, table, width, dot):
        need("fac", p)
        total = None
        for q in range(slots):
            picks = [ref[table[p, q, j]] for ref in panels for j in range(width)]
            term = dot(jnp.concatenate(picks, axis=0), fac[p, q])
            total = term if total is None else total + term
        return total

    def turns(vals, me, count, sign):
        slots_left = list(range(1, len(vals)))
        far = []
        for k in slots_left:
            peer = lax.rem(me + (sign * vals[k] + count), count)
            far.append(jnp.abs(peer - me))
        ranks = []
        for i, k in enumerate(slots_left):
            rank = jnp.int32(0)
            for j in range(len(slots_left)):
                if j < i:
                    rank = rank + jnp.where(far[j] >= far[i], 1, 0)
                elif j > i:
                    rank = rank + jnp.where(far[j] > far[i], 1, 0)
            ranks.append(rank)
        picked = []
        for turn in range(len(slots_left)):
            k_now, v_now = jnp.int32(0), jnp.int32(0)
            for i, k in enumerate(slots_left):
                k_now = jnp.where(ranks[i] == turn, k, k_now)
                v_now = jnp.where(ranks[i] == turn, vals[k], v_now)
            picked.append((k_now, v_now))
        return picked

    row_out = turns(row_vals, me_r, n_row, 1)
    row_back = turns(row_vals, me_r, n_row, -1)

    def spread(phase, h, vals, device, total, part, recv):
        for k in order(vals):
            part[k] = total[k * rows : (k + 1) * rows].astype(jnp.bfloat16)
            if device is col_dev:
                send(phase, h, part.at[k], recv.at[k], device(vals[k]))
        if device is row_dev:
            for k, v in row_out:
                send(phase, h, part.at[k], recv.at[k], device(v))
        return total[:rows].astype(jnp.bfloat16).astype(jnp.float32)

    def collect(phase, h, recv, own, width):
        arrive(phase, h, recv, width)
        for k in range(1, width):
            own = own + recv[k].astype(jnp.float32)
        return own

    def share(phase, h, vals, device, panels):
        if device is row_dev:
            for k, v in row_back:
                send(phase, h, panels.at[0], panels.at[k], device(-v))
        else:
            for k in order(vals):
                send(phase, h, panels.at[0], panels.at[k], device(-vals[k]))

    everyone = range(streams)

    def part_of(h):
        return pl.ds(h * rows, rows)

    need("rhs", 0)
    need("inv", 0)
    y = dot_t(rhs[0].astype(jnp.bfloat16), inv[0])
    yfull[0] = y
    for h in everyone:
        ycol[h][0][0] = y[h * rows : (h + 1) * rows].astype(jnp.bfloat16)
    pl.semaphore_wait(barrier, row_w + col_w - 2)
    phase = 0
    for h in everyone:
        share(phase, h, col_vals, col_dev, ycol[h][0])

    zero = jnp.zeros((rows, rhs.shape[2]), jnp.bfloat16)
    for h in everyone:
        for lvl in range(levels - 1):
            ycol[h][lvl][col_w] = zero
            brow[h][lvl + 1][row_w] = zero
    need("tgt", 0)
    need("src", 0)
    for p in range(len(pairs)):
        for q in range(slots):
            off_r = tgt_ref[p, 0, q] - me_r
            off_c = src_ref[p, 0, q] - me_c
            off_r = jnp.where(off_r < 0, off_r + n_row, off_r)
            off_c = jnp.where(off_c < 0, off_c + n_col, off_c)
            pos_r = jnp.int32(0)
            for k in range(1, row_w):
                pos_r = jnp.where(off_r == row_vals[k], k, pos_r)
            pos_c = jnp.int32(0)
            for k in range(1, col_w):
                pos_c = jnp.where(off_c == col_vals[k], k, pos_c)
            for k in range(row_w):
                ftab[p, q, k] = jnp.where(pos_r == k, pos_c, col_w)
            for k in range(col_w):
                btab[p, q, k] = jnp.where(pos_c == k, pos_r, row_w)

    for k in range(1, levels):
        near = pairs.index((k, k - 1))
        own = [None] * streams
        for h in everyone:
            arrive(phase, h, ycol[h][k - 1], col_w)
            total = product(near, [ycol[h][k - 1]], ftab, row_w, dot_t)
            if k > 1:
                total = total + facc[k, pl.ds(h * row_w * rows, row_w * rows)]
            own[h] = spread(
                phase + 1, h, row_vals, row_dev, total, fpart.at[h, k], frecv.at[h, k]
            )
        for p, (d, s) in enumerate(pairs):
            if s == k - 1 and d > k:
                later = product(p, [ycol[h][s] for h in everyone], ftab, row_w, dot_t)
                facc[d] = later if s == 0 else facc[d] + later
        need("rhs", k)
        need("inv", k)
        answers = [None] * streams
        for h in everyone:
            fsum = collect(phase + 1, h, frecv.at[h, k], own[h], row_w)
            y = dot_t((rhs[k, part_of(h)] - fsum).astype(jnp.bfloat16), inv[k])
            ybf = y.astype(jnp.bfloat16)
            if k < levels - 1:
                ycol[h][k][0] = ybf
                share(phase + 2, h, col_vals, col_dev, ycol[h][k])
                yfull[k, part_of(h)] = y
            else:
                answers[h] = dot_n(ybf, inv[k])
                brow[h][k][0] = answers[h].astype(jnp.bfloat16)
                share(phase + 2, h, row_vals, row_dev, brow[h][k])
                out_ref[k, 0, 0, part_of(h)] = answers[h]
        phase += 2

    top = levels - 1
    for k in reversed(range(top)):
        near = pairs.index((k + 1, k))
        own = [None] * streams
        for h in everyone:
            arrive(phase, h, brow[h][k + 1], row_w)
            total = product(near, [brow[h][k + 1]], btab, col_w, dot_n)
            if k + 1 < top:
                total = total + bacc[k, pl.ds(h * col_w * rows, col_w * rows)]
            own[h] = spread(
                phase + 1, h, col_vals, col_dev, total, bpart.at[h, k], brecv.at[h, k]
            )
        for p, (d, s) in enumerate(pairs):
            if d == k + 1 and s < k:
                later = product(p, [brow[h][d] for h in everyone], btab, col_w, dot_n)
                bacc[s] = later if d == top else bacc[s] + later
        for h in everyone:
            bsum = collect(phase + 1, h, brecv.at[h, k], own[h], col_w)
            answer = dot_n((yfull[k, part_of(h)] - bsum).astype(jnp.bfloat16), inv[k])
            if k > 0:
                brow[h][k][0] = answer.astype(jnp.bfloat16)
                share(phase + 2, h, row_vals, row_dev, brow[h][k])
            out_ref[k, 0, 0, part_of(h)] = answer
        phase += 2
    panels_sent = (levels - 1) * 2 * (row_w + col_w - 2)
    sent = fac.at[0, pl.ds(0, panels_sent * rhs.shape[1] // fac.shape[2])]
    pltpu.make_async_copy(sent, sent, send_sem.at[0]).wait()


def shards(n_row, n_col, rhs, inv, fac, tgt, src):
    levels, nrhs, size = rhs.shape[0], rhs.shape[3], rhs.shape[4]
    pairs, slots = fac.shape[0], fac.shape[2]
    row_w = len(offset_choices(WINDOW, n_row))
    col_w = len(offset_choices(WINDOW, n_col))
    phases = 4 * (levels - 1)
    rows = nrhs // STREAMS
    bf, f32 = jnp.bfloat16, jnp.float32
    return pl.pallas_call(
        functools.partial(kernel, n_row, n_col),
        out_shape=pltpu.VMEM(rhs.shape, f32),
        in_specs=[pl.BlockSpec(memory_space=pl.ANY)] * 5,
        out_specs=pl.BlockSpec(memory_space=pltpu.VMEM),
        scratch_shapes=[
            pltpu.VMEM((levels, nrhs, size), f32),
            pltpu.VMEM((levels, size, size), bf),
            pltpu.VMEM((pairs, slots, size, size), bf),
            [[pltpu.VMEM((col_w + 1, rows, size), bf)] * (levels - 1)] * STREAMS,
            [[pltpu.VMEM((row_w + 1, rows, size), bf)] * levels] * STREAMS,
            pltpu.VMEM((STREAMS, levels, row_w, rows, size), bf),
            pltpu.VMEM((STREAMS, levels, row_w, rows, size), bf),
            pltpu.VMEM((STREAMS, levels - 1, col_w, rows, size), bf),
            pltpu.VMEM((STREAMS, levels - 1, col_w, rows, size), bf),
            pltpu.VMEM((levels - 1, nrhs, size), f32),
            pltpu.VMEM((levels, row_w * nrhs, size), f32),
            pltpu.VMEM((levels - 1, col_w * nrhs, size), f32),
            pltpu.SMEM(tgt.shape, jnp.int32),
            pltpu.SMEM(src.shape, jnp.int32),
            pltpu.SMEM((pairs, slots, row_w), jnp.int32),
            pltpu.SMEM((pairs, slots, col_w), jnp.int32),
            pltpu.SemaphoreType.DMA((2,)),
            pltpu.SemaphoreType.DMA((levels,)),
            pltpu.SemaphoreType.DMA((levels,)),
            pltpu.SemaphoreType.DMA((pairs,)),
            pltpu.SemaphoreType.DMA((1,)),
            pltpu.SemaphoreType.DMA((phases, STREAMS)),
        ],
        compiler_params=pltpu.CompilerParams(collective_id=0, has_side_effects=True),
    )(rhs, inv, fac, tgt, src)


def solution(mesh):
    placed = (
        P(None, "row", "col", None, None),
        P(None, "row", "col", None, None),
        P(None, "row", "col", None, None),
        P(None, "row", "col"),
        P(None, "row", "col"),
    )
    return jax.shard_map(
        functools.partial(shards, mesh.shape["row"], mesh.shape["col"]),
        mesh=mesh,
        in_specs=placed,
        out_specs=P(None, "row", "col", None, None),
        check_vma=False,
    )
```
